32 devices in a mesh: seq: 16 (over z, y, core), ctx: 2 (over x).
Axes of the slice: x: 2, y: 2, z: 4, core: 2. Of those that a mesh axis runs over, the one named last changes fastest.
Arguments:
- tokens: bfloat16 [16, 256, 896], P('seq', 'ctx'), may hold values from -6 to 6
- positions: int32 [16, 256], P('seq'), may hold values from 0 to 255, as said below
- cotangent: bfloat16 [16, 256, 896], P('seq', 'ctx'), may hold values from -6 to 6
- qkv_weight: bfloat16 [896, 1152], P('seq'), may hold values from -0.1875 to 0.1875
- qkv_bias: bfloat16 [1152], P('seq'), may hold values from -16 to 16
- out_weight: bfloat16 [896, 896], P('seq'), may hold values from -0.75 to 0.75
- gate_up_weight: bfloat16 [896, 9728], P('seq'), may hold values from -0.1875 to 0.1875
- down_weight: bfloat16 [4864, 896], P('seq'), may hold values from -0.078125 to 0.078125
- attn_gain: bfloat16 [896], P('seq'), may hold values from 0.099609375 to 1.8984375
- ffn_gain: bfloat16 [896], P('seq'), may hold values from 0.099609375 to 1.8984375
Outputs:
- output: bfloat16 [16, 256, 896], P('seq', 'ctx')
- input_grad: float32 [16, 256, 896], P('seq', 'ctx')
- qkv_weight_grad: float32 [896, 1152], P('seq')
- qkv_bias_grad: float32 [1152], P('seq')
- out_weight_grad: float32 [896, 896], P('seq')
- gate_up_weight_grad: float32 [896, 9728], P('seq')
- down_weight_grad: float32 [4864, 896], P('seq')
- attn_gain_grad: float32 [896], P('seq')
- ffn_gain_grad: float32 [896], P('seq')
The draws below stay inside these ranges and needn't reach their ends.
Inputs may be any that keep to these rules, and one draw needn't show every extreme that they name: Each sequence holds every position of 0 to 255 once. The 128 stored tokens of one index of ctx are two blocks of 64 consecutive positions in rising order, block b and block 3 - b, with b drawn for each sequence.
All inputs are finite; a program needn't handle non-finite values.
Results may differ from the reference program's by a relative error of at most 0.018.
The reference program's roundings to bfloat16 on the way count: a program that leaves them out, or rounds other values in their place, can miss the bound.
Values may be sent and summed in bfloat16 or wider, within the bound.
A program may use at most 192 MiB of HBM per device.

```python
import jax
import jax.numpy as jnp
from jax import lax

D = 896
HEADS = 14
KV_HEADS = 2
HEAD_DIM = 64
FF = 4864
SPAN = 64
LEN = 256
SEQS = 16
QKV = 1152
N_CTX = 2


def draw_positions(key, part):
    seq_keys = jax.random.split(key, SEQS)
    orders = jax.vmap(lambda one_key: jax.random.permutation(one_key, N_CTX))(seq_keys)
    offsets = jnp.arange(SPAN, dtype=jnp.int32)
    first_half = orders[:, :, None] * SPAN + offsets[None, None, :]
    second_half = (2 * N_CTX - 1 - orders[:, :, None]) * SPAN + offsets[None, None, :]
    joined = jnp.concatenate([first_half, second_half], axis=2)
    return joined.reshape(SEQS, LEN).astype(jnp.int32)


def draw_qkv_bias(key, part):
    columns = (HEADS + 2 * KV_HEADS) * HEAD_DIM
    normal_draw = jax.random.normal(key, (columns,), jnp.float32)
    return jnp.clip(normal_draw * 0.5, -2.5, 2.5).astype(jnp.bfloat16)


def levels(key, dims, cuts, low, largest):
    def one(axis_at, shards_of):
        steps = jax.random.uniform(jax.random.fold_in(jax.random.fold_in(key, 6), axis_at), (shards_of,), jnp.float32, low / len(cuts), largest / len(cuts))
        return jnp.repeat(jnp.exp(steps), dims[axis_at] // shards_of).reshape((-1,) + (1,) * (len(dims) - axis_at - 1))

    gain = one(*cuts[0])
    for cut in cuts[1:]:
        gain = gain * one(*cut)
    return gain


def noise(key, dims, spread, most, cuts=(), held_as=jnp.bfloat16):
    factor_of = levels(key, dims, cuts, -0.22, 0.18) if cuts else 1.0
    values = jax.random.normal(key, dims, jnp.float32) * spread * factor_of
    return jnp.minimum(jnp.maximum(values, -most), most).astype(held_as)


def setup_inputs(seed: int = 0) -> dict:
    seeds = jax.random.split(jax.random.key(seed), 11)
    return {
        "tokens": noise(seeds[0], (SEQS, LEN, D), 1.0, 6.0, ((0, 16), (1, 2))),
        "positions": draw_positions(jax.random.fold_in(seeds[10], 71), 0),
        "cotangent": noise(seeds[2], (SEQS, LEN, D), 1.0, 6.0, ((0, 16), (1, 2))),
        "qkv_weight": noise(seeds[3], (D, QKV), D ** -0.5, 0.1875, ((0, 16),)),
        "qkv_bias": draw_qkv_bias(jax.random.fold_in(seeds[10], 71), 0),
        "out_weight": noise(seeds[5], (HEADS * HEAD_DIM, D), (HEADS * HEAD_DIM // 16) ** -0.5, 0.75, ((0, 16),)),
        "gate_up_weight": noise(seeds[6], (D, 2 * FF), D ** -0.5, 0.1875, ((0, 16),)),
        "down_weight": noise(seeds[7], (FF, D), FF ** -0.5, 0.078125, ((0, 16),)),
        "attn_gain": jnp.clip(1.0 + 0.18 * jax.random.normal(seeds[8], (D,), jnp.float32), 0.099609375, 1.8984375).astype(jnp.bfloat16),
        "ffn_gain": jnp.clip(1.0 + 0.18 * jax.random.normal(seeds[9], (D,), jnp.float32), 0.099609375, 1.8984375).astype(jnp.bfloat16),
    }


EPS = 1e-06
ROPE_BASE = 1000000.0

def to_bf16(values):
    return lax.optimization_barrier(values.astype(jnp.bfloat16))

def rope_tables(position_row):
    half_dim = HEAD_DIM // 2
    exponent = jnp.arange(half_dim, dtype=jnp.float32) * (2.0 / HEAD_DIM)
    inverse = ROPE_BASE ** (-exponent)
    angles = position_row.astype(jnp.float32)[:, None] * inverse[None, :]
    cosine_table = jnp.cos(angles)
    sine_table = jnp.sin(angles)
    return (jnp.concatenate([cosine_table, cosine_table], -1), jnp.concatenate([sine_table, sine_table], -1))

def rotate_half(values):
    half_dim = values.shape[-1] // 2
    return jnp.concatenate([-values[..., half_dim:], values[..., :half_dim]], -1)

def rotate_back(values):
    half_dim = values.shape[-1] // 2
    return jnp.concatenate([values[..., half_dim:], -values[..., :half_dim]], -1)

def rms_forward(values):
    scaling = lax.rsqrt(lax.optimization_barrier(jnp.mean(values * values, axis=-1, keepdims=True)) + EPS)
    return (values * scaling, scaling)

def rms_backward(grad_normed, normed, scaling, gain_float):
    gain_grad = lax.optimization_barrier(jnp.sum(grad_normed * normed, axis=0))
    grad_scaled = grad_normed * gain_float
    inner = lax.optimization_barrier(jnp.mean(grad_scaled * normed, axis=-1, keepdims=True))
    return (scaling * (grad_scaled - normed * inner), gain_grad)

def sequence_pass(token_row, position_row, cot_row, weights):
    full_qkv, full_bias, full_out, full_gate_up, full_down, gain_one, gain_two = weights
    row_count = token_row.shape[0]
    group_size = HEADS // KV_HEADS
    query_width = HEADS * HEAD_DIM
    key_width = KV_HEADS * HEAD_DIM
    score_scale = HEAD_DIM ** (-0.5)
    f32 = jnp.float32
    inputs_f = token_row.astype(f32)
    gain_one_f = gain_one.astype(f32)
    gain_two_f = gain_two.astype(f32)
    normed_one, scale_one = rms_forward(inputs_f)
    first_in = to_bf16(normed_one * gain_one_f)
    projected = jnp.dot(first_in, full_qkv, preferred_element_type=f32) + full_bias.astype(f32)
    cosine_table, sine_table = rope_tables(position_row)
    cos_query = cosine_table[:, None, None, :]
    sin_query = sine_table[:, None, None, :]
    cos_key = cosine_table[:, None, :]
    sin_key = sine_table[:, None, :]
    query = projected[:, :query_width].reshape(row_count, KV_HEADS, group_size, HEAD_DIM)
    keys = projected[:, query_width:query_width + key_width].reshape(row_count, KV_HEADS, HEAD_DIM)
    values = projected[:, query_width + key_width:].reshape(row_count, KV_HEADS, HEAD_DIM)
    query_rot = to_bf16(query * cos_query + rotate_half(query) * sin_query)
    key_rot = to_bf16(keys * cos_key + rotate_half(keys) * sin_key)
    value_b = to_bf16(values)
    scores = jnp.einsum('tkgd,skd->kgts', query_rot.astype(f32), key_rot.astype(f32)) * score_scale
    allowed = position_row[None, :] <= position_row[:, None]
    scores = jnp.where(allowed, scores, -1e+30)
    row_top = lax.optimization_barrier(jnp.max(scores, axis=-1, keepdims=True))
    log_total = row_top + jnp.log(lax.optimization_barrier(jnp.sum(jnp.exp(scores - row_top), axis=-1, keepdims=True)))
    probs = jnp.exp(scores - log_total)
    probs_b = to_bf16(probs)
    attended = to_bf16(jnp.einsum('kgts,skd->tkgd', probs_b.astype(f32), value_b.astype(f32)))
    attended_flat = attended.reshape(row_count, query_width)
    residual = inputs_f + jnp.dot(attended_flat, full_out, preferred_element_type=f32)
    normed_two, scale_two = rms_forward(residual)
    second_in = to_bf16(normed_two * gain_two_f)
    gate_up = jnp.dot(second_in, full_gate_up, preferred_element_type=f32)
    gate = gate_up[:, :FF]
    upward = gate_up[:, FF:]
    activated = to_bf16(jax.nn.silu(gate) * upward)
    output_row = (residual + jnp.dot(activated, full_down, preferred_element_type=f32)).astype(jnp.bfloat16)
    down_grad = jnp.dot(activated.T, cot_row, preferred_element_type=f32)
    grad_act = jnp.dot(cot_row, full_down.T, preferred_element_type=f32)
    sigmoid_gate = jax.nn.sigmoid(gate)
    grad_gate = grad_act * upward * sigmoid_gate * (1.0 + gate * (1.0 - sigmoid_gate))
    grad_upward = grad_act * jax.nn.silu(gate)
    grad_gate_up = to_bf16(jnp.concatenate([grad_gate, grad_upward], -1))
    gate_up_grad = jnp.dot(second_in.T, grad_gate_up, preferred_element_type=f32)
    grad_second = jnp.dot(grad_gate_up, full_gate_up.T, preferred_element_type=f32)
    grad_through, gain_two_grad = rms_backward(grad_second, normed_two, scale_two, gain_two_f)
    grad_residual = cot_row.astype(f32) + grad_through
    grad_res_b = to_bf16(grad_residual)
    out_grad = jnp.dot(attended_flat.T, grad_res_b, preferred_element_type=f32)
    grad_attended = to_bf16(jnp.dot(grad_res_b, full_out.T, preferred_element_type=f32))
    grad_attended = grad_attended.reshape(row_count, KV_HEADS, group_size, HEAD_DIM)
    grad_probs = jnp.einsum('tkgd,skd->kgts', grad_attended.astype(f32), value_b.astype(f32))
    delta = lax.optimization_barrier(jnp.sum(grad_attended.astype(f32) * attended.astype(f32), axis=-1))
    delta = jnp.transpose(delta, (1, 2, 0))[..., None]
    grad_scores = to_bf16(probs * (grad_probs - delta) * score_scale)
    grad_query_rot = jnp.einsum('kgts,skd->tkgd', grad_scores.astype(f32), key_rot.astype(f32))
    grad_key_rot = jnp.einsum('kgts,tkgd->skd', grad_scores.astype(f32), query_rot.astype(f32))
    grad_value = jnp.einsum('kgts,tkgd->skd', probs_b.astype(f32), grad_attended.astype(f32))
    grad_query = grad_query_rot * cos_query + rotate_back(grad_query_rot * sin_query)
    grad_key = grad_key_rot * cos_key + rotate_back(grad_key_rot * sin_key)
    grad_projected = jnp.concatenate([grad_query.reshape(row_count, query_width), grad_key.reshape(row_count, key_width), grad_value.reshape(row_count, key_width)], -1)
    bias_grad = lax.optimization_barrier(jnp.sum(grad_projected, axis=0))
    grad_proj_b = to_bf16(grad_projected)
    qkv_grad = jnp.dot(first_in.T, grad_proj_b, preferred_element_type=f32)
    grad_first = jnp.dot(grad_proj_b, full_qkv.T, preferred_element_type=f32)
    grad_input_part, gain_one_grad = rms_backward(grad_first, normed_one, scale_one, gain_one_f)
    input_row_grad = grad_residual + grad_input_part
    grads = (qkv_grad, bias_grad, out_grad, gate_up_grad, down_grad, gain_one_grad, gain_two_grad)
    return (output_row, input_row_grad, grads)

def reference(tokens, positions, cotangent, qkv_weight, qkv_bias, out_weight, gate_up_weight, down_weight, attn_gain, ffn_gain):
    weights = (qkv_weight, qkv_bias, out_weight, gate_up_weight, down_weight, attn_gain, ffn_gain)
    totals = tuple((jnp.zeros(weight.shape, jnp.float32) for weight in weights))

    def step_sequence(carried, inputs_row):
        token_row, position_row, cot_row = inputs_row
        output_row, input_row_grad, grads = sequence_pass(token_row, position_row, cot_row, weights)
        return (jax.tree.map(jnp.add, carried, grads), (output_row, input_row_grad))
    sums, (outputs, input_grads) = lax.scan(step_sequence, totals, (tokens, positions, cotangent))
    return (outputs, input_grads, sums[0], sums[1], sums[2], sums[3], sums[4], sums[5], sums[6])
```

```python
import jax
import jax.numpy as jnp
from jax import lax
from jax.sharding import PartitionSpec as P

HEADS = 14
KV_HEADS = 2
HEAD_DIM = 64


EPS = 1e-06
ROPE_BASE = 1000000.0


def to_bf16(values):
    return lax.optimization_barrier(values.astype(jnp.bfloat16))


def rope_tables(position_row):
    half_dim = HEAD_DIM // 2
    exponent = jnp.arange(half_dim, dtype=jnp.float32) * (2.0 / HEAD_DIM)
    inverse = ROPE_BASE ** (-exponent)
    angles = position_row.astype(jnp.float32)[:, None] * inverse[None, :]
    cosine_table = jnp.cos(angles)
    sine_table = jnp.sin(angles)
    return (
        jnp.concatenate([cosine_table, cosine_table], -1),
        jnp.concatenate([sine_table, sine_table], -1),
    )


def rotate_half(values):
    half_dim = values.shape[-1] // 2
    return jnp.concatenate([-values[..., half_dim:], values[..., :half_dim]], -1)


def rotate_back(values):
    half_dim = values.shape[-1] // 2
    return jnp.concatenate([values[..., half_dim:], -values[..., :half_dim]], -1)


def rms_forward(values):
    scaling = lax.rsqrt(jnp.mean(values * values, axis=-1, keepdims=True) + EPS)
    return (values * scaling, scaling)


def rms_backward(grad_normed, normed, scaling, gain_float):
    gain_grad = jnp.sum(grad_normed * normed, axis=0)
    grad_scaled = grad_normed * gain_float
    inner = jnp.mean(grad_scaled * normed, axis=-1, keepdims=True)
    return (scaling * (grad_scaled - normed * inner), gain_grad)


def weight_rows(left_side, right_side):
    return lax.psum_scatter(
        lax.dot_general(
            left_side, right_side, (((0,), (0,)), ((), ())), preferred_element_type=jnp.float32
        ),
        "seq",
        scatter_dimension=0,
        tiled=True,
    )


def columns_from_rows(rows, parts):
    depth = rows.shape[0]
    hidden = rows.shape[1] // (2 * parts)
    split = jnp.transpose(rows.reshape(depth, 2, parts, hidden), (2, 0, 1, 3))
    split = split.reshape(parts, depth, 2 * hidden)
    moved = lax.all_to_all(split, "seq", split_axis=0, concat_axis=0, tiled=True)
    return moved.reshape(parts * depth, 2 * hidden)


def rows_from_columns(columns, parts):
    depth = columns.shape[0] // parts
    hidden = columns.shape[1] // 2
    split = columns.reshape(parts, depth, 2 * hidden)
    moved = lax.all_to_all(split, "seq", split_axis=0, concat_axis=0, tiled=True)
    moved = jnp.transpose(moved.reshape(parts, depth, 2, hidden), (1, 2, 0, 3))
    return moved.reshape(depth, 2 * parts * hidden)


def contract_rows(left_side, right_side):
    return lax.dot_general(
        left_side, right_side, (((0,), (0,)), ((), ())), preferred_element_type=jnp.float32
    )


def contract_columns(left_side, right_side):
    return lax.dot_general(
        left_side, right_side, (((1,), (1,)), ((), ())), preferred_element_type=jnp.float32
    )


def scatter_tokens(partial):
    return lax.psum_scatter(partial, "seq", scatter_dimension=0, tiled=True)


def shards(
    tokens,
    positions,
    cotangent,
    qkv_weight,
    qkv_bias,
    out_weight,
    gate_up_weight,
    down_weight,
    attn_gain,
    ffn_gain,
):
    f32 = jnp.float32
    gathered = (
        lax.all_gather(qkv_weight, "seq", axis=0, tiled=True),
        lax.all_gather(qkv_bias, "seq", axis=0, tiled=True),
        lax.all_gather(out_weight, "seq", axis=0, tiled=True),
        lax.all_gather(attn_gain, "seq", axis=0, tiled=True),
        lax.all_gather(ffn_gain, "seq", axis=0, tiled=True),
    )
    full_qkv, full_bias, full_out, gain_one, gain_two = gathered
    parts = lax.axis_size("seq")
    hidden = down_weight.shape[0]
    own_gate_up = columns_from_rows(gate_up_weight, parts)
    all_cot = lax.all_gather(cotangent[0], "seq", axis=0, tiled=True)
    inputs_f = tokens[0].astype(f32)
    cot_row = cotangent[0]
    row_count = inputs_f.shape[0]
    group_size = HEADS // KV_HEADS
    query_width = HEADS * HEAD_DIM
    key_width = KV_HEADS * HEAD_DIM
    score_scale = HEAD_DIM ** (-0.5)
    all_positions = positions[0]
    position_row = lax.dynamic_slice_in_dim(
        all_positions, lax.axis_index("ctx") * row_count, row_count, 0
    )
    normed_one, scale_one = rms_forward(inputs_f)
    first_in = to_bf16(normed_one * gain_one.astype(f32))
    projected = jnp.dot(first_in, full_qkv, preferred_element_type=f32) + full_bias.astype(f32)
    cosine_table, sine_table = rope_tables(position_row)
    cos_query = cosine_table[:, None, None, :]
    sin_query = sine_table[:, None, None, :]
    cos_key = cosine_table[:, None, :]
    sin_key = sine_table[:, None, :]
    query = projected[:, :query_width].reshape(row_count, KV_HEADS, group_size, HEAD_DIM)
    keys = projected[:, query_width : query_width + key_width].reshape(
        row_count, KV_HEADS, HEAD_DIM
    )
    values = projected[:, query_width + key_width :]
    query_rot = to_bf16(query * cos_query + rotate_half(query) * sin_query)
    key_rot = to_bf16(keys * cos_key + rotate_half(keys) * sin_key).reshape(row_count, key_width)
    value_b = to_bf16(values)
    all_keys, all_values = (
        lax.all_gather(key_rot, "ctx", axis=0, tiled=True),
        lax.all_gather(value_b, "ctx", axis=0, tiled=True),
    )
    all_keys = all_keys.reshape(-1, KV_HEADS, HEAD_DIM)
    all_values = all_values.reshape(-1, KV_HEADS, HEAD_DIM)
    scores = (
        jnp.einsum("tkgd,skd->kgts", query_rot, all_keys, preferred_element_type=f32) * score_scale
    )
    allowed = all_positions[None, :] <= position_row[:, None]
    scores = jnp.where(allowed, scores, -1e30)
    row_top = jnp.max(scores, axis=-1, keepdims=True)
    log_total = row_top + jnp.log(jnp.sum(jnp.exp(scores - row_top), axis=-1, keepdims=True))
    probs = jnp.exp(scores - log_total)
    probs_b = to_bf16(probs)
    attended = to_bf16(
        jnp.einsum("kgts,skd->tkgd", probs_b, all_values, preferred_element_type=f32)
    )
    attended_flat = attended.reshape(row_count, query_width)
    residual = inputs_f + jnp.dot(attended_flat, full_out, preferred_element_type=f32)
    normed_two, scale_two = rms_forward(residual)
    second_in = to_bf16(normed_two * gain_two.astype(f32))
    all_second = lax.all_gather(second_in, "seq", axis=0, tiled=True)
    gate_up = jnp.dot(all_second, own_gate_up, preferred_element_type=f32)
    gate = gate_up[:, :hidden]
    upward = gate_up[:, hidden:]
    sigmoid_gate = jax.nn.sigmoid(gate)
    activated = to_bf16(gate * sigmoid_gate * upward)
    grad_act = contract_columns(all_cot, down_weight)
    grad_gate = grad_act * upward * sigmoid_gate * (1.0 + gate * (1.0 - sigmoid_gate))
    grad_upward = grad_act * (gate * sigmoid_gate)
    grad_gate_up = to_bf16(jnp.concatenate([grad_gate, grad_upward], -1))
    grad_second = scatter_tokens(contract_columns(grad_gate_up, own_gate_up))
    output_row = (
        residual + scatter_tokens(jnp.dot(activated, down_weight, preferred_element_type=f32))
    ).astype(jnp.bfloat16)
    down_grad = contract_rows(activated, all_cot)
    gate_up_grad = rows_from_columns(contract_rows(all_second, grad_gate_up), parts)
    grad_through, gain_two_grad = rms_backward(
        grad_second, normed_two, scale_two, gain_two.astype(f32)
    )
    grad_residual = cot_row.astype(f32) + grad_through
    grad_res_b = to_bf16(grad_residual)
    out_grad = weight_rows(attended_flat, grad_res_b)
    grad_attended = to_bf16(jnp.dot(grad_res_b, full_out.T, preferred_element_type=f32))
    grad_attended = grad_attended.reshape(row_count, KV_HEADS, group_size, HEAD_DIM)
    grad_probs = jnp.einsum("tkgd,skd->kgts", grad_attended, all_values, preferred_element_type=f32)
    delta = jnp.sum(grad_attended.astype(f32) * attended.astype(f32), axis=-1)
    delta = jnp.transpose(delta, (1, 2, 0))[..., None]
    grad_scores = to_bf16(probs * (grad_probs - delta) * score_scale)
    grad_query_rot = jnp.einsum("kgts,skd->tkgd", grad_scores, all_keys, preferred_element_type=f32)
    key_part = jnp.einsum("kgts,tkgd->skd", grad_scores, query_rot, preferred_element_type=f32)
    value_part = jnp.einsum("kgts,tkgd->skd", probs_b, grad_attended, preferred_element_type=f32)
    key_local = lax.psum_scatter(
        jnp.concatenate(
            [
                key_part.reshape(row_count * lax.axis_size("ctx"), key_width),
                value_part.reshape(row_count * lax.axis_size("ctx"), key_width),
            ],
            -1,
        ),
        "ctx",
        scatter_dimension=0,
        tiled=True,
    )
    grad_key_rot = key_local[:, :key_width].reshape(row_count, KV_HEADS, HEAD_DIM)
    grad_value = key_local[:, key_width:]
    grad_query = grad_query_rot * cos_query + rotate_back(grad_query_rot * sin_query)
    grad_key = grad_key_rot * cos_key + rotate_back(grad_key_rot * sin_key)
    grad_projected = jnp.concatenate(
        [
            grad_query.reshape(row_count, query_width),
            grad_key.reshape(row_count, key_width),
            grad_value,
        ],
        -1,
    )
    bias_grad = jnp.sum(grad_projected, axis=0)
    grad_proj_b = to_bf16(grad_projected)
    qkv_grad = weight_rows(first_in, grad_proj_b)
    grad_first = jnp.dot(grad_proj_b, full_qkv.T, preferred_element_type=f32)
    grad_input_part, gain_one_grad = rms_backward(
        grad_first, normed_one, scale_one, gain_one.astype(f32)
    )
    input_row_grad = grad_residual + grad_input_part
    bias_share, gain_one_share, gain_two_share = (
        lax.psum_scatter(bias_grad, "seq", scatter_dimension=0, tiled=True),
        lax.psum_scatter(gain_one_grad, "seq", scatter_dimension=0, tiled=True),
        lax.psum_scatter(gain_two_grad, "seq", scatter_dimension=0, tiled=True),
    )
    summed = lax.psum(
        (qkv_grad, bias_share, out_grad, gate_up_grad, down_grad, gain_one_share, gain_two_share),
        "ctx",
    )
    (
        result_qkv,
        result_bias,
        result_out,
        result_gate_up,
        result_down,
        result_gain_one,
        result_gain_two,
    ) = summed
    return (
        output_row[None],
        input_row_grad[None],
        result_qkv,
        result_bias,
        result_out,
        result_gate_up,
        result_down,
        result_gain_one,
        result_gain_two,
    )


def solution(mesh):
    in_specs = (
        P("seq", "ctx", None),
        P("seq", None),
        P("seq", "ctx", None),
        P("seq", None),
        P("seq"),
        P("seq", None),
        P("seq", None),
        P("seq", None),
        P("seq"),
        P("seq"),
    )
    out_specs = (
        P("seq", "ctx", None),
        P("seq", "ctx", None),
        P("seq", None),
        P("seq"),
        P("seq", None),
        P("seq", None),
        P("seq", None),
        P("seq"),
        P("seq"),
    )
    return jax.shard_map(shards, mesh=mesh, in_specs=in_specs, out_specs=out_specs, check_vma=False)
```

```python
import jax
import jax.numpy as jnp
from jax import lax
from jax.sharding import PartitionSpec as P

HEADS = 14
KV_HEADS = 2
HEAD_DIM = 64


EPS = 1e-06
ROPE_BASE = 1000000.0


def to_bf16(values):
    return lax.optimization_barrier(values.astype(jnp.bfloat16))


def rope_tables(position_row):
    half_dim = HEAD_DIM // 2
    exponent = jnp.arange(half_dim, dtype=jnp.float32) * (2.0 / HEAD_DIM)
    inverse = ROPE_BASE ** (-exponent)
    angles = position_row.astype(jnp.float32)[:, None] * inverse[None, :]
    cosine_table = jnp.cos(angles)
    sine_table = jnp.sin(angles)
    return (
        jnp.concatenate([cosine_table, cosine_table], -1),
        jnp.concatenate([sine_table, sine_table], -1),
    )


def rotate_half(values):
    half_dim = values.shape[-1] // 2
    return jnp.concatenate([-values[..., half_dim:], values[..., :half_dim]], -1)


def rotate_back(values):
    half_dim = values.shape[-1] // 2
    return jnp.concatenate([values[..., half_dim:], -values[..., :half_dim]], -1)


def rms_forward(values):
    scaling = lax.rsqrt(jnp.mean(values * values, axis=-1, keepdims=True) + EPS)
    return (values * scaling, scaling)


def rms_backward(grad_normed, normed, scaling, gain_float):
    gain_grad = jnp.sum(grad_normed * normed, axis=0)
    grad_scaled = grad_normed * gain_float
    inner = jnp.mean(grad_scaled * normed, axis=-1, keepdims=True)
    return (scaling * (grad_scaled - normed * inner), gain_grad)


def weight_rows(left_side, right_side):
    return lax.psum_scatter(
        lax.dot_general(
            left_side, right_side, (((0,), (0,)), ((), ())), preferred_element_type=jnp.float32
        ),
        "seq",
        scatter_dimension=0,
        tiled=True,
    )


def columns_from_rows(rows, parts):
    depth = rows.shape[0]
    hidden = rows.shape[1] // (2 * parts)
    split = jnp.transpose(rows.reshape(depth, 2, parts, hidden), (2, 0, 1, 3))
    split = split.reshape(parts, depth, 2 * hidden)
    moved = lax.all_to_all(split, "seq", split_axis=0, concat_axis=0, tiled=True)
    return moved.reshape(parts * depth, 2 * hidden)


def rows_from_columns(columns, parts):
    depth = columns.shape[0] // parts
    hidden = columns.shape[1] // 2
    split = columns.reshape(parts, depth, 2 * hidden)
    moved = lax.all_to_all(split, "seq", split_axis=0, concat_axis=0, tiled=True)
    moved = jnp.transpose(moved.reshape(parts, depth, 2, hidden), (1, 2, 0, 3))
    return moved.reshape(depth, 2 * parts * hidden)


def contract_rows(left_side, right_side):
    return lax.dot_general(
        left_side, right_side, (((0,), (0,)), ((), ())), preferred_element_type=jnp.float32
    )


def contract_columns(left_side, right_side):
    return lax.dot_general(
        left_side, right_side, (((1,), (1,)), ((), ())), preferred_element_type=jnp.float32
    )


def scatter_tokens(partial):
    total = lax.psum_scatter(to_bf16(partial), "seq", scatter_dimension=0, tiled=True)
    return total.astype(jnp.float32)


def packed_height(depth):
    return (depth + 16) // 16 * 16


def other(values):
    return lax.ppermute(values, "ctx", [(0, 1), (1, 0)])


def sum_rounded(values):
    if lax.axis_size("ctx") != 2:
        return lax.psum(values, "ctx")
    mine = to_bf16(values)
    return mine.astype(jnp.float32) + other(mine).astype(jnp.float32)


def sum_ctx(values):
    if lax.axis_size("ctx") != 2:
        return lax.psum(values, "ctx")
    return values + other(values)


def shards(
    tokens,
    positions,
    cotangent,
    qkv_weight,
    qkv_bias,
    out_weight,
    gate_up_weight,
    down_weight,
    attn_gain,
    ffn_gain,
):
    f32 = jnp.float32
    qkv_columns = qkv_weight.shape[1]
    depth = qkv_weight.shape[0]
    bias_count = qkv_bias.shape[0]
    packed_rows = packed_height(depth)
    pair = jnp.concatenate([qkv_weight, out_weight], 1)
    extra = jnp.concatenate([qkv_bias, attn_gain, ffn_gain])
    extra = jnp.pad(extra, (0, pair.shape[1] - extra.shape[0]))[None]
    packed = jnp.concatenate(
        [pair, extra, jnp.zeros((packed_rows - depth - 1, pair.shape[1]), pair.dtype)], 0
    )
    packed = lax.all_gather(packed, "seq", axis=0, tiled=True).reshape(-1, packed_rows, pair.shape[1])
    full_qkv = packed[:, :depth, :qkv_columns].reshape(-1, qkv_columns)
    full_out = packed[:, :depth, qkv_columns:].reshape(-1, out_weight.shape[1])
    full_bias = packed[:, depth, :bias_count].reshape(-1)
    gain_one = packed[:, depth, bias_count : bias_count + depth].reshape(-1)
    gain_two = packed[:, depth, bias_count + depth : bias_count + 2 * depth].reshape(-1)
    parts = lax.axis_size("seq")
    hidden = down_weight.shape[0]
    own_gate_up = columns_from_rows(gate_up_weight, parts)
    own_gate_up, full_qkv = lax.optimization_barrier((own_gate_up, full_qkv))
    all_cot = lax.all_gather(cotangent[0], "seq", axis=0, tiled=True)
    inputs_f = tokens[0].astype(f32)
    cot_row = cotangent[0]
    row_count = inputs_f.shape[0]
    group_size = HEADS // KV_HEADS
    query_width = HEADS * HEAD_DIM
    key_width = KV_HEADS * HEAD_DIM
    score_scale = HEAD_DIM ** (-0.5)
    all_positions = positions[0]
    position_row = lax.dynamic_slice_in_dim(
        all_positions, lax.axis_index("ctx") * row_count, row_count, 0
    )
    normed_one, scale_one = rms_forward(inputs_f)
    first_in = to_bf16(normed_one * gain_one.astype(f32))
    projected = jnp.dot(first_in, full_qkv, preferred_element_type=f32) + full_bias.astype(f32)
    cosine_table, sine_table = rope_tables(position_row)
    cos_query = cosine_table[:, None, None, :]
    sin_query = sine_table[:, None, None, :]
    cos_key = cosine_table[:, None, :]
    sin_key = sine_table[:, None, :]
    query = projected[:, :query_width].reshape(row_count, KV_HEADS, group_size, HEAD_DIM)
    keys = projected[:, query_width : query_width + key_width].reshape(
        row_count, KV_HEADS, HEAD_DIM
    )
    values = projected[:, query_width + key_width :]
    query_rot = to_bf16(query * cos_query + rotate_half(query) * sin_query)
    key_rot = to_bf16(keys * cos_key + rotate_half(keys) * sin_key).reshape(row_count, key_width)
    value_b = to_bf16(values)
    both = jnp.concatenate([key_rot, value_b], -1)
    if lax.axis_size("ctx") == 2:
        both = jnp.concatenate([both, other(both)], 0)
        other_row = lax.dynamic_slice_in_dim(
            all_positions, (1 - lax.axis_index("ctx")) * row_count, row_count, 0
        )
        all_positions = jnp.concatenate([position_row, other_row])
    else:
        both = lax.all_gather(both, "ctx", axis=0, tiled=True)
    all_keys, all_values = both[:, :key_width], both[:, key_width:]
    all_keys = all_keys.reshape(-1, KV_HEADS, HEAD_DIM)
    all_values = all_values.reshape(-1, KV_HEADS, HEAD_DIM)
    scores = (
        jnp.einsum("tkgd,skd->kgts", query_rot, all_keys, preferred_element_type=f32) * score_scale
    )
    allowed = all_positions[None, :] <= position_row[:, None]
    scores = jnp.where(allowed, scores, -1e30)
    row_top = jnp.max(scores, axis=-1, keepdims=True)
    log_total = row_top + jnp.log(jnp.sum(jnp.exp(scores - row_top), axis=-1, keepdims=True))
    probs = jnp.exp(scores - log_total)
    probs_b = to_bf16(probs)
    attended = to_bf16(
        jnp.einsum("kgts,skd->tkgd", probs_b, all_values, preferred_element_type=f32)
    )
    attended_flat = attended.reshape(row_count, query_width)
    residual = inputs_f + jnp.dot(attended_flat, full_out, preferred_element_type=f32)
    normed_two, scale_two = rms_forward(residual)
    second_in = to_bf16(normed_two * gain_two.astype(f32))
    all_second = lax.all_gather(second_in, "seq", axis=0, tiled=True)
    gate_up = jnp.dot(all_second, own_gate_up, preferred_element_type=f32)
    gate = gate_up[:, :hidden]
    upward = gate_up[:, hidden:]
    sigmoid_gate = jax.nn.sigmoid(gate)
    activated = to_bf16(gate * sigmoid_gate * upward)
    grad_act = contract_columns(all_cot, down_weight)
    grad_gate = grad_act * upward * sigmoid_gate * (1.0 + gate * (1.0 - sigmoid_gate))
    grad_upward = grad_act * (gate * sigmoid_gate)
    grad_gate_up = to_bf16(jnp.concatenate([grad_gate, grad_upward], -1))
    grad_second = scatter_tokens(contract_columns(grad_gate_up, own_gate_up))
    output_row = (
        residual + scatter_tokens(jnp.dot(activated, down_weight, preferred_element_type=f32))
    ).astype(jnp.bfloat16)
    result_down = sum_rounded(contract_rows(activated, all_cot))
    result_gate_up = rows_from_columns(
        to_bf16(sum_rounded(contract_rows(all_second, grad_gate_up))), parts
    ).astype(f32)
    grad_through, gain_two_grad = rms_backward(
        grad_second, normed_two, scale_two, gain_two.astype(f32)
    )
    grad_residual = cot_row.astype(f32) + grad_through
    grad_res_b = to_bf16(grad_residual)
    out_grad = weight_rows(attended_flat, grad_res_b)
    grad_attended = to_bf16(jnp.dot(grad_res_b, full_out.T, preferred_element_type=f32))
    grad_attended = grad_attended.reshape(row_count, KV_HEADS, group_size, HEAD_DIM)
    grad_probs = jnp.einsum("tkgd,skd->kgts", grad_attended, all_values, preferred_element_type=f32)
    delta = jnp.sum(grad_attended.astype(f32) * attended.astype(f32), axis=-1)
    delta = jnp.transpose(delta, (1, 2, 0))[..., None]
    grad_scores = to_bf16(probs * (grad_probs - delta) * score_scale)
    grad_query_rot = jnp.einsum("kgts,skd->tkgd", grad_scores, all_keys, preferred_element_type=f32)
    key_part = jnp.einsum("kgts,tkgd->skd", grad_scores, query_rot, preferred_element_type=f32)
    value_part = jnp.einsum("kgts,tkgd->skd", probs_b, grad_attended, preferred_element_type=f32)
    key_parts = jnp.concatenate(
        [
            key_part.reshape(row_count * lax.axis_size("ctx"), key_width),
            value_part.reshape(row_count * lax.axis_size("ctx"), key_width),
        ],
        -1,
    )
    if lax.axis_size("ctx") == 2:
        key_local = key_parts[:row_count] + other(key_parts[row_count:])
    else:
        key_local = lax.psum_scatter(key_parts, "ctx", scatter_dimension=0, tiled=True)
    grad_key_rot = key_local[:, :key_width].reshape(row_count, KV_HEADS, HEAD_DIM)
    grad_value = key_local[:, key_width:]
    grad_query = grad_query_rot * cos_query + rotate_back(grad_query_rot * sin_query)
    grad_key = grad_key_rot * cos_key + rotate_back(grad_key_rot * sin_key)
    grad_projected = jnp.concatenate(
        [
            grad_query.reshape(row_count, query_width),
            grad_key.reshape(row_count, key_width),
            grad_value,
        ],
        -1,
    )
    bias_grad = jnp.sum(grad_projected, axis=0)
    grad_proj_b = to_bf16(grad_projected)
    grad_first = jnp.dot(grad_proj_b, full_qkv.T, preferred_element_type=f32)
    grad_input_part, gain_one_grad = rms_backward(
        grad_first, normed_one, scale_one, gain_one.astype(f32)
    )
    input_row_grad = grad_residual + grad_input_part
    small = jnp.concatenate(
        [
            bias_grad.reshape(parts, -1),
            gain_one_grad.reshape(parts, -1),
            gain_two_grad.reshape(parts, -1),
        ],
        -1,
    )
    small = jnp.pad(small, ((0, 0), (0, qkv_columns - small.shape[1])))[:, None]
    grad_rows = (depth + 8) // 8 * 8
    packed_grad = jnp.concatenate(
        [
            contract_rows(first_in, grad_proj_b).reshape(parts, depth, qkv_columns),
            small,
            jnp.zeros((parts, grad_rows - depth - 1, qkv_columns), f32),
        ],
        1,
    ).reshape(parts * grad_rows, qkv_columns)
    packed_sum = sum_ctx(lax.psum_scatter(packed_grad, "seq", scatter_dimension=0, tiled=True))
    result_qkv = packed_sum[:depth]
    result_bias = packed_sum[depth, :bias_count]
    result_gain_one = packed_sum[depth, bias_count : bias_count + depth]
    result_gain_two = packed_sum[depth, bias_count + depth : bias_count + 2 * depth]
    result_out = sum_ctx(out_grad)
    return (
        output_row[None],
        input_row_grad[None],
        result_qkv,
        result_bias,
        result_out,
        result_gate_up,
        result_down,
        result_gain_one,
        result_gain_two,
    )


def solution(mesh):
    in_specs = (
        P("seq", "ctx", None),
        P("seq", None),
        P("seq", "ctx", None),
        P("seq", None),
        P("seq"),
        P("seq", None),
        P("seq", None),
        P("seq", None),
        P("seq"),
        P("seq"),
    )
    out_specs = (
        P("seq", "ctx", None),
        P("seq", "ctx", None),
        P("seq", None),
        P("seq"),
        P("seq", None),
        P("seq", None),
        P("seq", None),
        P("seq"),
        P("seq"),
    )
    return jax.shard_map(shards, mesh=mesh, in_specs=in_specs, out_specs=out_specs, check_vma=False)
```

```python
import functools

import jax
import jax.numpy as jnp
from jax import lax
from jax.experimental import pallas as pl
from jax.experimental.pallas import tpu as pltpu
from jax.sharding import PartitionSpec as P

HEADS = 14
KV_HEADS = 2
HEAD_DIM = 64


EPS = 1e-06
ROPE_BASE = 1000000.0


def to_bf16(values):
    return lax.optimization_barrier(values.astype(jnp.bfloat16))


def rope_tables(position_row):
    half_dim = HEAD_DIM // 2
    exponent = jnp.arange(half_dim, dtype=jnp.float32) * (2.0 / HEAD_DIM)
    inverse = ROPE_BASE ** (-exponent)
    angles = position_row.astype(jnp.float32)[:, None] * inverse[None, :]
    cosine_table = jnp.cos(angles)
    sine_table = jnp.sin(angles)
    return (
        jnp.concatenate([cosine_table, cosine_table], -1),
        jnp.concatenate([sine_table, sine_table], -1),
    )


def rotate_half(values):
    half_dim = values.shape[-1] // 2
    return jnp.concatenate([-values[..., half_dim:], values[..., :half_dim]], -1)


def rotate_back(values):
    half_dim = values.shape[-1] // 2
    return jnp.concatenate([values[..., half_dim:], -values[..., :half_dim]], -1)


def rms_forward(values):
    scaling = lax.rsqrt(jnp.mean(values * values, axis=-1, keepdims=True) + EPS)
    return (values * scaling, scaling)


def rms_backward(grad_normed, normed, scaling, gain_float):
    gain_grad = jnp.sum(grad_normed * normed, axis=0)
    grad_scaled = grad_normed * gain_float
    inner = jnp.mean(grad_scaled * normed, axis=-1, keepdims=True)
    return (scaling * (grad_scaled - normed * inner), gain_grad)


def weight_rows(left_side, right_side):
    return lax.psum_scatter(
        lax.dot_general(
            left_side, right_side, (((0,), (0,)), ((), ())), preferred_element_type=jnp.float32
        ),
        "seq",
        scatter_dimension=0,
        tiled=True,
    )


def columns_from_rows(rows, parts):
    depth = rows.shape[0]
    hidden = rows.shape[1] // (2 * parts)
    split = jnp.transpose(rows.reshape(depth, 2, parts, hidden), (2, 0, 1, 3))
    split = split.reshape(parts, depth, 2 * hidden)
    moved = lax.all_to_all(split, "seq", split_axis=0, concat_axis=0, tiled=True)
    return moved.reshape(parts * depth, 2 * hidden)


def rows_from_columns(columns, parts):
    depth = columns.shape[0] // parts
    hidden = columns.shape[1] // 2
    split = columns.reshape(parts, depth, 2 * hidden)
    moved = lax.all_to_all(split, "seq", split_axis=0, concat_axis=0, tiled=True)
    moved = jnp.transpose(moved.reshape(parts, depth, 2, hidden), (1, 2, 0, 3))
    return moved.reshape(depth, 2 * parts * hidden)


def contract_rows(left_side, right_side):
    return lax.dot_general(
        left_side, right_side, (((0,), (0,)), ((), ())), preferred_element_type=jnp.float32
    )


def contract_columns(left_side, right_side):
    return lax.dot_general(
        left_side, right_side, (((1,), (1,)), ((), ())), preferred_element_type=jnp.float32
    )


def scatter_tokens(partial):
    total = lax.psum_scatter(to_bf16(partial), "seq", scatter_dimension=0, tiled=True)
    return total.astype(jnp.float32)


def gather_kernel(outer, own_ref, all_ref, local_sem, outer_sems, middle_sems, core_sems):
    me = lax.axis_index("seq")
    at_outer = me // 4
    middle = (me // 2) % 2
    core = me % 2
    rows = own_ref.shape[0]

    def place(outer_at, middle_at, core_at):
        index = outer_at * 4 + middle_at * 2 + core_at
        return all_ref.at[pl.ds(pl.multiple_of(index * rows, rows), rows)]

    def remote(source, target, sems, slot, device):
        return pltpu.make_async_remote_copy(
            src_ref=source,
            dst_ref=target,
            send_sem=sems.at[0, slot],
            recv_sem=sems.at[1, slot],
            device_id={"seq": device},
            device_id_type=pl.DeviceIdType.MESH,
        )

    middle_partner = at_outer * 4 + (1 - middle) * 2 + core
    core_partner = at_outer * 4 + middle * 2 + (1 - core)
    outer_partners = [
        ((at_outer + step) % outer) * 4 + middle * 2 + core for step in range(1, outer)
    ]
    barrier = pltpu.get_barrier_semaphore()
    for device in [middle_partner, core_partner] + outer_partners:
        pl.semaphore_signal(
            barrier, inc=1, device_id={"seq": device}, device_id_type=pl.DeviceIdType.MESH
        )
    pl.semaphore_wait(barrier, outer + 1)

    own_place = place(at_outer, middle, core)
    local = pltpu.make_async_copy(own_ref, own_place, local_sem)
    local.start()
    started = []
    outer_copies = []
    for step in range(1, outer):
        copy = remote(own_ref, own_place, outer_sems, step - 1, outer_partners[step - 1])
        copy.start()
        outer_copies.append(copy)
    middle_copies = []
    for step in range(outer):
        source_outer = (at_outer + outer - step) % outer
        here = place(source_outer, middle, core)
        if step == 0:
            source = own_ref
        else:
            outer_copies[step - 1].wait_recv()
            source = here
        copy = remote(source, here, middle_sems, step, middle_partner)
        copy.start()
        middle_copies.append(copy)
        copy = remote(source, here, core_sems, 2 * step, core_partner)
        copy.start()
        started.append(copy)
    for step in range(outer):
        source_outer = (at_outer + outer - step) % outer
        middle_copies[step].wait_recv()
        here = place(source_outer, 1 - middle, core)
        copy = remote(here, here, core_sems, 2 * step + 1, core_partner)
        copy.start()
        started.append(copy)
    for copy in started:
        copy.wait_recv()
    for copy in outer_copies + middle_copies + started:
        copy.wait_send()
    local.wait()


def gather_rows(rows, collective_id):
    parts = lax.axis_size("seq")
    if parts % 4:
        return lax.all_gather(rows, "seq", axis=0, tiled=True)
    outer = parts // 4
    return pl.pallas_call(
        functools.partial(gather_kernel, outer),
        out_shape=jax.ShapeDtypeStruct((parts * rows.shape[0], rows.shape[1]), rows.dtype),
        in_specs=[pl.BlockSpec(memory_space=pltpu.VMEM)],
        out_specs=pl.BlockSpec(memory_space=pltpu.VMEM),
        scratch_shapes=[
            pltpu.SemaphoreType.DMA,
            pltpu.SemaphoreType.DMA((2, max(outer - 1, 1))),
            pltpu.SemaphoreType.DMA((2, outer)),
            pltpu.SemaphoreType.DMA((2, 2 * outer)),
        ],
        compiler_params=pltpu.CompilerParams(
            collective_id=collective_id, has_side_effects=True, vmem_limit_bytes=24 * 2**20
        ),
    )(rows)


def packed_height(depth):
    return (depth + 16) // 16 * 16


def other(values):
    return lax.ppermute(values, "ctx", [(0, 1), (1, 0)])


def sum_rounded(values):
    if lax.axis_size("ctx") != 2:
        return lax.psum(values, "ctx")
    mine = to_bf16(values)
    return mine.astype(jnp.float32) + other(mine).astype(jnp.float32)


def sum_ctx(values):
    if lax.axis_size("ctx") != 2:
        return lax.psum(values, "ctx")
    return values + other(values)


def shards(
    tokens,
    positions,
    cotangent,
    qkv_weight,
    qkv_bias,
    out_weight,
    gate_up_weight,
    down_weight,
    attn_gain,
    ffn_gain,
):
    f32 = jnp.float32
    qkv_columns = qkv_weight.shape[1]
    depth = qkv_weight.shape[0]
    bias_count = qkv_bias.shape[0]
    packed_rows = packed_height(depth)
    pair = jnp.concatenate([qkv_weight, out_weight], 1)
    extra = jnp.concatenate([qkv_bias, attn_gain, ffn_gain])
    extra = jnp.pad(extra, (0, pair.shape[1] - extra.shape[0]))[None]
    packed = jnp.concatenate(
        [pair, extra, jnp.zeros((packed_rows - depth - 1, pair.shape[1]), pair.dtype)], 0
    )
    packed = lax.all_gather(packed, "seq", axis=0, tiled=True).reshape(-1, packed_rows, pair.shape[1])
    full_qkv = packed[:, :depth, :qkv_columns].reshape(-1, qkv_columns)
    full_out = packed[:, :depth, qkv_columns:].reshape(-1, out_weight.shape[1])
    full_bias = packed[:, depth, :bias_count].reshape(-1)
    gain_one = packed[:, depth, bias_count : bias_count + depth].reshape(-1)
    gain_two = packed[:, depth, bias_count + depth : bias_count + 2 * depth].reshape(-1)
    parts = lax.axis_size("seq")
    hidden = down_weight.shape[0]
    own_gate_up = columns_from_rows(gate_up_weight, parts)
    all_cot = gather_rows(cotangent[0], 0)
    own_gate_up, all_cot, full_qkv = lax.optimization_barrier((own_gate_up, all_cot, full_qkv))
    inputs_f = tokens[0].astype(f32)
    cot_row = cotangent[0]
    row_count = inputs_f.shape[0]
    group_size = HEADS // KV_HEADS
    query_width = HEADS * HEAD_DIM
    key_width = KV_HEADS * HEAD_DIM
    score_scale = HEAD_DIM ** (-0.5)
    all_positions = positions[0]
    position_row = lax.dynamic_slice_in_dim(
        all_positions, lax.axis_index("ctx") * row_count, row_count, 0
    )
    normed_one, scale_one = rms_forward(inputs_f)
    first_in = to_bf16(normed_one * gain_one.astype(f32))
    projected = jnp.dot(first_in, full_qkv, preferred_element_type=f32) + full_bias.astype(f32)
    cosine_table, sine_table = rope_tables(position_row)
    cos_query = cosine_table[:, None, None, :]
    sin_query = sine_table[:, None, None, :]
    cos_key = cosine_table[:, None, :]
    sin_key = sine_table[:, None, :]
    query = projected[:, :query_width].reshape(row_count, KV_HEADS, group_size, HEAD_DIM)
    keys = projected[:, query_width : query_width + key_width].reshape(
        row_count, KV_HEADS, HEAD_DIM
    )
    values = projected[:, query_width + key_width :]
    query_rot = to_bf16(query * cos_query + rotate_half(query) * sin_query)
    key_rot = to_bf16(keys * cos_key + rotate_half(keys) * sin_key).reshape(row_count, key_width)
    value_b = to_bf16(values)
    both = jnp.concatenate([key_rot, value_b], -1)
    if lax.axis_size("ctx") == 2:
        both = jnp.concatenate([both, other(both)], 0)
        other_row = lax.dynamic_slice_in_dim(
            all_positions, (1 - lax.axis_index("ctx")) * row_count, row_count, 0
        )
        all_positions = jnp.concatenate([position_row, other_row])
    else:
        both = lax.all_gather(both, "ctx", axis=0, tiled=True)
    all_keys, all_values = both[:, :key_width], both[:, key_width:]
    all_keys = all_keys.reshape(-1, KV_HEADS, HEAD_DIM)
    all_values = all_values.reshape(-1, KV_HEADS, HEAD_DIM)
    scores = (
        jnp.einsum("tkgd,skd->kgts", query_rot, all_keys, preferred_element_type=f32) * score_scale
    )
    allowed = all_positions[None, :] <= position_row[:, None]
    scores = jnp.where(allowed, scores, -1e30)
    row_top = jnp.max(scores, axis=-1, keepdims=True)
    log_total = row_top + jnp.log(jnp.sum(jnp.exp(scores - row_top), axis=-1, keepdims=True))
    probs = jnp.exp(scores - log_total)
    probs_b = to_bf16(probs)
    attended = to_bf16(
        jnp.einsum("kgts,skd->tkgd", probs_b, all_values, preferred_element_type=f32)
    )
    attended_flat = attended.reshape(row_count, query_width)
    residual = inputs_f + jnp.dot(attended_flat, full_out, preferred_element_type=f32)
    normed_two, scale_two = rms_forward(residual)
    second_in = to_bf16(normed_two * gain_two.astype(f32))
    all_second = gather_rows(second_in, 1)
    gate_up = jnp.dot(all_second, own_gate_up, preferred_element_type=f32)
    gate = gate_up[:, :hidden]
    upward = gate_up[:, hidden:]
    sigmoid_gate = jax.nn.sigmoid(gate)
    activated = to_bf16(gate * sigmoid_gate * upward)
    grad_act = contract_columns(all_cot, down_weight)
    grad_gate = grad_act * upward * sigmoid_gate * (1.0 + gate * (1.0 - sigmoid_gate))
    grad_upward = grad_act * (gate * sigmoid_gate)
    grad_gate_up = to_bf16(jnp.concatenate([grad_gate, grad_upward], -1))
    grad_second = scatter_tokens(contract_columns(grad_gate_up, own_gate_up))
    output_row = (
        residual + scatter_tokens(jnp.dot(activated, down_weight, preferred_element_type=f32))
    ).astype(jnp.bfloat16)
    result_down = sum_rounded(contract_rows(activated, all_cot))
    result_gate_up = rows_from_columns(
        to_bf16(sum_rounded(contract_rows(all_second, grad_gate_up))), parts
    ).astype(f32)
    grad_through, gain_two_grad = rms_backward(
        grad_second, normed_two, scale_two, gain_two.astype(f32)
    )
    grad_residual = cot_row.astype(f32) + grad_through
    grad_res_b = to_bf16(grad_residual)
    out_grad = weight_rows(attended_flat, grad_res_b)
    grad_attended = to_bf16(jnp.dot(grad_res_b, full_out.T, preferred_element_type=f32))
    grad_attended = grad_attended.reshape(row_count, KV_HEADS, group_size, HEAD_DIM)
    grad_probs = jnp.einsum("tkgd,skd->kgts", grad_attended, all_values, preferred_element_type=f32)
    delta = jnp.sum(grad_attended.astype(f32) * attended.astype(f32), axis=-1)
    delta = jnp.transpose(delta, (1, 2, 0))[..., None]
    grad_scores = to_bf16(probs * (grad_probs - delta) * score_scale)
    grad_query_rot = jnp.einsum("kgts,skd->tkgd", grad_scores, all_keys, preferred_element_type=f32)
    key_part = jnp.einsum("kgts,tkgd->skd", grad_scores, query_rot, preferred_element_type=f32)
    value_part = jnp.einsum("kgts,tkgd->skd", probs_b, grad_attended, preferred_element_type=f32)
    key_parts = jnp.concatenate(
        [
            key_part.reshape(row_count * lax.axis_size("ctx"), key_width),
            value_part.reshape(row_count * lax.axis_size("ctx"), key_width),
        ],
        -1,
    )
    if lax.axis_size("ctx") == 2:
        key_local = key_parts[:row_count] + other(key_parts[row_count:])
    else:
        key_local = lax.psum_scatter(key_parts, "ctx", scatter_dimension=0, tiled=True)
    grad_key_rot = key_local[:, :key_width].reshape(row_count, KV_HEADS, HEAD_DIM)
    grad_value = key_local[:, key_width:]
    grad_query = grad_query_rot * cos_query + rotate_back(grad_query_rot * sin_query)
    grad_key = grad_key_rot * cos_key + rotate_back(grad_key_rot * sin_key)
    grad_projected = jnp.concatenate(
        [
            grad_query.reshape(row_count, query_width),
            grad_key.reshape(row_count, key_width),
            grad_value,
        ],
        -1,
    )
    bias_grad = jnp.sum(grad_projected, axis=0)
    grad_proj_b = to_bf16(grad_projected)
    grad_first = jnp.dot(grad_proj_b, full_qkv.T, preferred_element_type=f32)
    grad_input_part, gain_one_grad = rms_backward(
        grad_first, normed_one, scale_one, gain_one.astype(f32)
    )
    input_row_grad = grad_residual + grad_input_part
    small = jnp.concatenate(
        [
            bias_grad.reshape(parts, -1),
            gain_one_grad.reshape(parts, -1),
            gain_two_grad.reshape(parts, -1),
        ],
        -1,
    )
    small = jnp.pad(small, ((0, 0), (0, qkv_columns - small.shape[1])))[:, None]
    grad_rows = (depth + 8) // 8 * 8
    packed_grad = jnp.concatenate(
        [
            contract_rows(first_in, grad_proj_b).reshape(parts, depth, qkv_columns),
            small,
            jnp.zeros((parts, grad_rows - depth - 1, qkv_columns), f32),
        ],
        1,
    ).reshape(parts * grad_rows, qkv_columns)
    packed_sum = sum_ctx(lax.psum_scatter(packed_grad, "seq", scatter_dimension=0, tiled=True))
    result_qkv = packed_sum[:depth]
    result_bias = packed_sum[depth, :bias_count]
    result_gain_one = packed_sum[depth, bias_count : bias_count + depth]
    result_gain_two = packed_sum[depth, bias_count + depth : bias_count + 2 * depth]
    result_out = sum_ctx(out_grad)
    return (
        output_row[None],
        input_row_grad[None],
        result_qkv,
        result_bias,
        result_out,
        result_gate_up,
        result_down,
        result_gain_one,
        result_gain_two,
    )


def solution(mesh):
    in_specs = (
        P("seq", "ctx", None),
        P("seq", None),
        P("seq", "ctx", None),
        P("seq", None),
        P("seq"),
        P("seq", None),
        P("seq", None),
        P("seq", None),
        P("seq"),
        P("seq"),
    )
    out_specs = (
        P("seq", "ctx", None),
        P("seq", "ctx", None),
        P("seq", None),
        P("seq"),
        P("seq", None),
        P("seq", None),
        P("seq", None),
        P("seq"),
        P("seq"),
    )
    return jax.shard_map(shards, mesh=mesh, in_specs=in_specs, out_specs=out_specs, check_vma=False)
```
